32 devices in a mesh: ia: 8 (over z, y), ja: 4 (over x, core).
Axes of the slice: x: 2, y: 2, z: 4, core: 2. Of those that a mesh axis runs over, the one named last changes fastest.
Arguments:
- basis: bfloat16 [16, 8, 1024, 256], P('ia', 'ja'), may hold values from -0.1875 to 0.1875
- amplitudes: float32 [16, 8, 256, 256], P('ia', 'ja'), may hold values from -6 to 6
- integrals: float32 [16, 8, 256, 256], P('ia', 'ja'), may hold values from -6 to 6
- virt_energy: float32 [1024], replicated, may hold values from 0.05 to 2
- fock: float32 [16, 16], replicated, may hold values from -3 to 3
- occ_energy: float32 [8], P('ja'), may hold values from -2 to -0.2
- blocks: int32 [16, 8], P(None, 'ja'), may hold values from 1 to 2
- couplings: int32 [16, 8, 4], P(None, 'ja'), may hold values from 0 to 15, as said below
Outputs:
- new_amplitudes: float32 [16, 8, 256, 256], P('ia', 'ja')
The draws below stay inside these ranges and needn't reach their ends.
Inputs may be any that keep to these rules, and one draw needn't show every extreme that they name: `couplings`: A pair's 4 entries name different k, none equal to the pair's own i, and no two in the same block of 2 consecutive first orbitals held by one index of ia. Of the 16 entries of the pairs that one device holds, exactly 2 name a k in each such block.
All inputs are finite; a program needn't handle non-finite values.
Results may differ from the reference program's by a relative error of at most 0.0031.
Values may be sent and summed in bfloat16 or wider, within the bound.
A program may use at most 128 MiB of HBM per device.

```python
import math
import jax
import jax.numpy as jnp
from jax import lax

NPROJ = 1024
NPNO = 256
BLOCK = 128
NCOUPLE = 4
OI_DEV = 2
OJ_DEV = 2
SWEEPS = 2
NI = 16
NJ = 8
N_IA = 8
N_JA = 4


def slot_order(slot_key):
    return jax.random.permutation(slot_key, NCOUPLE)


def draw_couplings(key, part):
    per_device = OI_DEV * OJ_DEV
    key_list = jax.random.split(key, N_IA * N_JA)
    row_ids = jnp.repeat(jnp.arange(N_IA, dtype=jnp.int32), N_JA)

    def one_device(device_key, row_group):
        split_keys = jax.random.split(device_key, 5)
        pair_order = jax.random.permutation(split_keys[0], per_device).astype(jnp.int32)
        within = jax.vmap(slot_order)(jax.random.split(split_keys[1], per_device)).astype(jnp.int32)
        position = NCOUPLE * pair_order[:, None] + within
        targets = jax.random.permutation(split_keys[2], N_IA).astype(jnp.int32)
        block_id = targets[position % N_IA]
        pair_row = (jnp.arange(per_device, dtype=jnp.int32) // OJ_DEV)[:, None]
        other_row = (pair_row + 1 + jax.random.randint(split_keys[3], (per_device, NCOUPLE), 0, OI_DEV - 1)) % OI_DEV
        any_row = jax.random.randint(split_keys[4], (per_device, NCOUPLE), 0, OI_DEV)
        offset_row = jnp.where(block_id == row_group, other_row, any_row)
        return (block_id * OI_DEV + offset_row).astype(jnp.int32).reshape(OI_DEV, OJ_DEV, NCOUPLE)
    pieces = jax.vmap(one_device)(key_list, row_ids)
    pieces = pieces.reshape(N_IA, N_JA, OI_DEV, OJ_DEV, NCOUPLE).transpose(0, 2, 1, 3, 4)
    return pieces.reshape(N_IA * OI_DEV, N_JA * OJ_DEV, NCOUPLE)


def touch_ends(array, rng, smallest, high):
    place = [jax.random.randint(jax.random.fold_in(rng, axis), (), 0, length) for axis, length in enumerate(array.shape)]
    longest = array.shape.index(max(array.shape))
    next_to = place[:longest] + [(place[longest] + 1) % array.shape[longest]] + place[longest + 1:]
    return array.at[tuple(place)].set(smallest).at[tuple(next_to)].set(high)


def steps_of(stream_key, dims, cuts, smallest, high):
    level, own = 1.0, jax.random.fold_in(stream_key, 6)
    for dim, parts in cuts:
        heights = jnp.exp(jax.random.uniform(jax.random.fold_in(own, dim), (parts,), jnp.float32, smallest / len(cuts), high / len(cuts)))
        level = level * jnp.repeat(heights, dims[dim] // parts).reshape([-1 if axis == dim else 1 for axis in range(len(dims))])
    return level


def gaussian(rng, shape, deviation, most, cuts=(), kind=jnp.bfloat16):
    values = deviation * jax.random.normal(rng, shape, jnp.float32)
    if cuts:
        values = values * steps_of(rng, shape, cuts, -0.22, 0.18)
    return jnp.clip(values, -most, most).astype(kind)


def setup_inputs(seed: int = 0) -> dict:
    streams_of = jax.random.split(jax.random.key(seed), 9)
    return {
        "basis": gaussian(streams_of[0], (NI, NJ, NPROJ, NPNO), NPROJ ** -0.5, 0.1875, ((0, 8), (1, 4))),
        "amplitudes": gaussian(streams_of[1], (NI, NJ, NPNO, NPNO), 1.0, 6.0, ((0, 8), (1, 4)), jnp.float32),
        "integrals": gaussian(streams_of[2], (NI, NJ, NPNO, NPNO), 1.0, 6.0, ((0, 8), (1, 4)), jnp.float32),
        "virt_energy": jnp.clip(jnp.exp(jax.random.uniform(streams_of[3], (NPROJ,), jnp.float32, math.log(0.05), math.log(2.0))), 0.05, 2.0),
        "fock": gaussian(streams_of[4], (NI, NI), 0.5, 3.0, (), jnp.float32),
        "occ_energy": jnp.clip(-2.0 + 1.8 * jax.random.uniform(streams_of[5], (NJ,), jnp.float32) ** steps_of(streams_of[5], (NJ,), ((0, 4),), -0.2, 0.2), -2.0, -0.2),
        "blocks": touch_ends(jax.random.randint(streams_of[6], (NI, NJ), 1, NPNO // BLOCK + 1), jax.random.fold_in(streams_of[6], 1), 1, (NPNO // BLOCK + 1) - 1).astype(jnp.int32),
        "couplings": draw_couplings(jax.random.fold_in(streams_of[8], 71), 0),
    }


clip_share = 0.4
denominator_floor = 1.0

def rounded_wide(values):
    return lax.optimization_barrier(values.astype(jnp.bfloat16)).astype(jnp.float32)

def reference(basis, amplitudes, integrals, virt_energy, fock, occ_energy, blocks, couplings):
    orbital_index = jnp.arange(NPNO, dtype=jnp.int32)
    column_mask = orbital_index[None, None, :] < (blocks * BLOCK)[:, :, None]
    masked = basis * column_mask[:, :, None, :].astype(jnp.bfloat16)
    pair_mask = (column_mask[:, :, :, None] & column_mask[:, :, None, :]).astype(jnp.float32)
    row_ids = jnp.arange(NI, dtype=jnp.int32)
    weights = fock[row_ids[:, None, None], couplings]
    energy_shift = jnp.diagonal(fock)[:, None] + occ_energy[None, :]
    pair_ids = jnp.arange(NI * NJ, dtype=jnp.int32)

    def prepare(pair_id):
        row_id = pair_id // NJ
        column_id = pair_id % NJ
        own_basis = masked[row_id, column_id].astype(jnp.float32)
        partners = masked[couplings[row_id, column_id], column_id].astype(jnp.float32)
        intersection = jnp.einsum('xa,sxb->sab', own_basis, partners, precision=lax.Precision.HIGHEST).astype(jnp.bfloat16)
        scaled = rounded_wide(own_basis * virt_energy[:, None])
        virtual = jnp.einsum('xa,xb->ab', own_basis, scaled, precision=lax.Precision.HIGHEST)
        return (intersection, virtual)
    intersections, virtuals = lax.map(prepare, pair_ids)
    diagonal_part = jnp.diagonal(virtuals, axis1=1, axis2=2).reshape(NI, NJ, NPNO)
    denominators = jnp.maximum(diagonal_part[:, :, :, None] + diagonal_part[:, :, None, :] - energy_shift[:, :, None, None], denominator_floor)
    current = amplitudes * pair_mask
    for sweep_index in range(SWEEPS):
        rounded = current.astype(jnp.bfloat16)

        def update_of(pair_id):
            row_id = pair_id // NJ
            column_id = pair_id % NJ
            intersection = intersections[pair_id].astype(jnp.float32)
            partner_amplitudes = rounded[couplings[row_id, column_id], column_id].astype(jnp.float32)
            first_product = rounded_wide(jnp.einsum('sab,sbc->sac', intersection, partner_amplitudes, precision=lax.Precision.HIGHEST))
            second_product = jnp.einsum('sac,sdc->sad', first_product, intersection, precision=lax.Precision.HIGHEST)
            coupled = jnp.einsum('sad,s->ad', second_product, weights[row_id, column_id], precision=lax.Precision.HIGHEST)
            amplitude_block = rounded[row_id, column_id].astype(jnp.float32)
            virtual_block = rounded_wide(virtuals[pair_id])
            local_terms = jnp.dot(virtual_block, amplitude_block, precision=lax.Precision.HIGHEST) + jnp.dot(amplitude_block, virtual_block, precision=lax.Precision.HIGHEST)
            residual = integrals[row_id, column_id] + local_terms - energy_shift[row_id, column_id] * current[row_id, column_id] - coupled
            return pair_mask[row_id, column_id] * residual / denominators[row_id, column_id]
        update = lax.map(update_of, pair_ids).reshape(NI, NJ, NPNO, NPNO)
        squares = jnp.sum(update * update)
        factor = jnp.minimum(1.0, clip_share * NPNO / jnp.sqrt(squares / (NI * NJ) + 1e-06))
        current = current - factor * update
    return current
```

```python
import functools

import jax
import jax.numpy as jnp
from jax import lax
from jax.experimental import pallas as pl
from jax.experimental.pallas import tpu as pltpu
from jax.sharding import PartitionSpec as P

BLOCK = 128
NCOUPLE = 4
SWEEPS = 2
MESH = pl.DeviceIdType.MESH

clip_share = 0.4
denominator_floor = 1.0


def rank_within(block_ids):
    entries = block_ids.shape[-1]
    matching = block_ids[..., :, None] == block_ids[..., None, :]
    earlier = jnp.arange(entries)[:, None] > jnp.arange(entries)[None, :]
    return jnp.sum((matching & earlier).astype(jnp.int32), axis=-1)


def total_kernel(n_ia, n_ja, x_ref, o_ref, near, far, near_send, near_recv, far_send, far_recv, own_sem):
    ia, ja = lax.axis_index("ia"), lax.axis_index("ja")
    barrier = pltpu.get_barrier_semaphore()
    for step in range(1, n_ja):
        pl.semaphore_signal(barrier, inc=1, device_id=(ia, lax.rem(ja + step, n_ja)), device_id_type=MESH)
    for step in range(1, n_ia):
        pl.semaphore_signal(barrier, inc=1, device_id=(lax.rem(ia + step, n_ia), ja), device_id_type=MESH)
    own = pltpu.make_async_copy(x_ref, near.at[0], own_sem)
    own.start()
    pl.semaphore_wait(barrier, n_ja + n_ia - 2)
    copies = []
    for step in range(1, n_ja):
        copy = pltpu.make_async_remote_copy(
            src_ref=x_ref,
            dst_ref=near.at[step],
            send_sem=near_send.at[step],
            recv_sem=near_recv.at[step],
            device_id=(ia, lax.rem(ja + step, n_ja)),
            device_id_type=MESH,
        )
        copy.start()
        copies.append(copy)
    own.wait()
    for copy in copies:
        copy.wait()
    copies = []
    for step in range(1, n_ia):
        copy = pltpu.make_async_remote_copy(
            src_ref=near,
            dst_ref=far.at[step - 1],
            send_sem=far_send.at[step],
            recv_sem=far_recv.at[step],
            device_id=(lax.rem(ia + step, n_ia), ja),
            device_id_type=MESH,
        )
        copy.start()
        copies.append(copy)
    for copy in copies:
        copy.wait()
    o_ref[...] = jnp.sum(near[...], axis=0) + jnp.sum(far[...].reshape(((n_ia - 1) * n_ja,) + o_ref.shape), axis=0)


def total_of(x, n_ia, n_ja, call):
    shape = x.shape
    return pl.pallas_call(
        functools.partial(total_kernel, n_ia, n_ja),
        out_shape=jax.ShapeDtypeStruct(shape, jnp.float32),
        in_specs=[pl.BlockSpec(memory_space=pltpu.VMEM)],
        out_specs=pl.BlockSpec(memory_space=pltpu.VMEM),
        scratch_shapes=[
            pltpu.VMEM((n_ja,) + shape, jnp.float32),
            pltpu.VMEM((n_ia - 1, n_ja) + shape, jnp.float32),
            pltpu.SemaphoreType.DMA((n_ja,)),
            pltpu.SemaphoreType.DMA((n_ja,)),
            pltpu.SemaphoreType.DMA((n_ia,)),
            pltpu.SemaphoreType.DMA((n_ia,)),
            pltpu.SemaphoreType.DMA,
        ],
        compiler_params=pltpu.CompilerParams(collective_id=call, has_side_effects=True),
        name="total" + str(call),
    )(x)


def live_rows(shape, live):
    return lax.broadcasted_iota(jnp.int32, shape, 0) < live


def live_columns(shape, live):
    return lax.broadcasted_iota(jnp.int32, shape, 1) < live


def virtual_kernel(live, shift, basis, energy, virtual, denominators):
    p = pl.program_id(0)
    width = basis.shape[2]
    own = basis[0]
    scaled = (own.astype(jnp.float32) * energy[...]).astype(jnp.bfloat16)
    full = jnp.dot(own.T, scaled, preferred_element_type=jnp.float32)
    both = live_rows(full.shape, live[p]) & live_columns(full.shape, live[p])
    full = jnp.where(both, full, 0.0)
    virtual[0] = full.astype(jnp.bfloat16)
    same = lax.broadcasted_iota(jnp.int32, full.shape, 0) == lax.broadcasted_iota(jnp.int32, full.shape, 1)
    picked = jnp.where(same, full, 0.0)
    down = jnp.sum(picked, axis=1, keepdims=True)
    across = jnp.sum(picked, axis=0, keepdims=True)
    denominators[0] = jnp.maximum(down + across - shift[p], denominator_floor)


def virtual_of(basis, energy, live, shift):
    pairs, projected, width = basis.shape
    return pl.pallas_call(
        virtual_kernel,
        out_shape=(
            jax.ShapeDtypeStruct((pairs, width, width), jnp.bfloat16),
            jax.ShapeDtypeStruct((pairs, width, width), jnp.float32),
        ),
        grid_spec=pltpu.PrefetchScalarGridSpec(
            num_scalar_prefetch=2,
            grid=(pairs,),
            in_specs=[
                pl.BlockSpec((1, projected, width), lambda p, *_: (p, 0, 0)),
                pl.BlockSpec((projected, 1), lambda p, *_: (0, 0)),
            ],
            out_specs=[pl.BlockSpec((1, width, width), lambda p, *_: (p, 0, 0))] * 2,
        ),
        cost_estimate=pl.CostEstimate(flops=2 * pairs * projected * width * width, bytes_accessed=4 * pairs * projected * width, transcendentals=0),
    )(live, shift, basis, energy)


def overlap_kernel(arrival, live, live_partner, own, partner, out, turned):
    p, s = pl.program_id(0), pl.program_id(1)

    @pl.when(s == 0)
    def _():
        turned[...] = own[0].T

    full = jnp.dot(turned[...], partner[0], preferred_element_type=jnp.float32)
    both = live_rows(full.shape, live[p]) & live_columns(full.shape, live_partner[p * NCOUPLE + s])
    out[0] = jnp.where(both, full, 0.0).astype(jnp.bfloat16)


def overlap_of(basis, arrived, arrival, live, live_partner):
    pairs, projected, width = basis.shape
    return pl.pallas_call(
        overlap_kernel,
        out_shape=jax.ShapeDtypeStruct((pairs * NCOUPLE, width, width), jnp.bfloat16),
        grid_spec=pltpu.PrefetchScalarGridSpec(
            num_scalar_prefetch=3,
            grid=(pairs, NCOUPLE),
            in_specs=[
                pl.BlockSpec((1, projected, width), lambda p, s, *_: (p, 0, 0)),
                pl.BlockSpec((1, projected, width), lambda p, s, a, *_: (a[p * NCOUPLE + s], 0, 0)),
            ],
            out_specs=pl.BlockSpec((1, width, width), lambda p, s, *_: (p * NCOUPLE + s, 0, 0)),
            scratch_shapes=[pltpu.VMEM((width, projected), jnp.bfloat16)],
        ),
    )(arrival, live, live_partner, basis, arrived)


def sweep_kernel(arrival, live, weights, shift, overlap, partner, virtual, denominators, current, integrals, update, squares, coupled):
    p, s = pl.program_id(0), pl.program_id(1)
    first = jnp.dot(overlap[0], partner[0], preferred_element_type=jnp.float32).astype(jnp.bfloat16)
    second = lax.dot_general(first, overlap[0], (((1,), (1,)), ((), ())), preferred_element_type=jnp.float32)
    term = weights[p * NCOUPLE + s] * second

    @pl.when(s == 0)
    def _():
        coupled[...] = term

    @pl.when(s > 0)
    def _():
        coupled[...] += term

    @pl.when(s == NCOUPLE - 1)
    def _():
        rounded = current[0].astype(jnp.bfloat16)
        residual = integrals[0] + jnp.dot(virtual[0], rounded, preferred_element_type=jnp.float32)
        residual = residual + jnp.dot(rounded, virtual[0], preferred_element_type=jnp.float32)
        residual = residual - shift[p] * current[0] - coupled[...]
        both = live_rows(residual.shape, live[p]) & live_columns(residual.shape, live[p])
        change = jnp.where(both, residual, 0.0) / denominators[0]
        update[0] = change
        squared = change * change
        height, width = squared.shape
        part = jnp.sum(squared.reshape(height // 8, 8, width), axis=0)
        folded = part[:, :128]
        for start in range(128, width, 128):
            folded = folded + part[:, start : start + 128]

        @pl.when(p == 0)
        def _():
            squares[...] = folded

        @pl.when(p > 0)
        def _():
            squares[...] += folded


def sweep_of(overlap, arrived, arrival, live, weights, shift, virtual, denominators, current, integrals):
    pairs, width, _ = current.shape
    wide = pl.BlockSpec((1, width, width), lambda p, s, *_: (p, 0, 0))
    return pl.pallas_call(
        sweep_kernel,
        out_shape=(
            jax.ShapeDtypeStruct((pairs, width, width), jnp.float32),
            jax.ShapeDtypeStruct((8, 128), jnp.float32),
        ),
        grid_spec=pltpu.PrefetchScalarGridSpec(
            num_scalar_prefetch=4,
            grid=(pairs, NCOUPLE),
            in_specs=[
                pl.BlockSpec((1, width, width), lambda p, s, *_: (p * NCOUPLE + s, 0, 0)),
                pl.BlockSpec((1, width, width), lambda p, s, a, *_: (a[p * NCOUPLE + s], 0, 0)),
                wide,
                wide,
                wide,
                wide,
            ],
            out_specs=[wide, pl.BlockSpec((8, 128), lambda p, s, *_: (0, 0))],
            scratch_shapes=[pltpu.VMEM((width, width), jnp.float32)],
        ),
    )(arrival, live, weights, shift, overlap, arrived, virtual, denominators, current, integrals)


def gather_kernel(sources, x, out):
    out[...] = x[...]


def gather_of(x, sources):
    count = sources.shape[0]
    rows, width = x.shape[1:]
    return pl.pallas_call(
        gather_kernel,
        out_shape=jax.ShapeDtypeStruct((count, rows, width), x.dtype),
        grid_spec=pltpu.PrefetchScalarGridSpec(
            num_scalar_prefetch=1,
            grid=(count,),
            in_specs=[pl.BlockSpec((1, rows, width), lambda n, a: (a[n], 0, 0))],
            out_specs=pl.BlockSpec((1, rows, width), lambda n, a: (n, 0, 0)),
        ),
    )(sources, x)


def shards(basis, amplitudes, integrals, virt_energy, fock, occ_energy, blocks, couplings):
    rows_here, columns_here, projected, pair_width = basis.shape
    pairs_here = rows_here * columns_here
    requests = NCOUPLE * pairs_here
    row_groups = lax.axis_size("ia")
    column_groups = lax.axis_size("ja")
    slot_count = requests // row_groups
    group_index = lax.axis_index("ia")
    first_row = group_index * rows_here
    total_pairs = rows_here * row_groups * columns_here * column_groups
    live = lax.dynamic_slice_in_dim(blocks, first_row, rows_here, 0).reshape(pairs_here) * BLOCK
    orbital_index = jnp.arange(pair_width, dtype=jnp.int32)
    column_mask = orbital_index[None, :] < live[:, None]
    pair_mask = column_mask[:, :, None] & column_mask[:, None, :]
    local_couplings = lax.dynamic_slice_in_dim(couplings, first_row, rows_here, 0)
    local_targets = local_couplings.reshape(requests) // rows_here
    arrival = local_targets * slot_count + rank_within(local_targets)
    all_couplings = couplings.reshape(row_groups, requests)
    all_targets = all_couplings // rows_here
    all_ranks = rank_within(all_targets)
    pair_column = jnp.arange(requests, dtype=jnp.int32) // NCOUPLE % columns_here
    source_pair = (all_couplings - first_row) * columns_here + pair_column[None, :]
    slot_index = jnp.arange(slot_count, dtype=jnp.int32)
    chosen = (all_targets == group_index)[:, :, None] & (
        all_ranks[:, :, None] == slot_index[None, None, :]
    )
    sources = jnp.sum(chosen.astype(jnp.int32) * source_pair[:, :, None], axis=1).reshape(
        row_groups * slot_count
    )
    fock_rows = lax.dynamic_slice_in_dim(fock, first_row, rows_here, 0)
    picked = local_couplings[:, :, :, None] == jnp.arange(fock.shape[1], dtype=jnp.int32)
    weights = jnp.sum(jnp.where(picked, fock_rows[:, None, None, :], 0.0), axis=-1).reshape(requests)
    live_partner = BLOCK * jnp.sum(
        jnp.where(picked, blocks.T[None, :, None, :], 0), axis=-1
    ).reshape(requests)
    occupied_diag = lax.dynamic_slice_in_dim(jnp.diagonal(fock), first_row, rows_here, 0)
    shift = (occupied_diag[:, None] + occ_energy[None, :]).reshape(pairs_here)
    bases = basis.reshape(pairs_here, projected, pair_width)
    current = jnp.where(pair_mask, amplitudes.reshape(pairs_here, pair_width, pair_width), 0.0)
    pair_integrals = integrals.reshape(pairs_here, pair_width, pair_width)
    arrived_bases = lax.all_to_all(
        gather_of(bases, sources), "ia", split_axis=0, concat_axis=0, tiled=True
    )
    virtual, denominators = virtual_of(bases, virt_energy[:, None], live, shift)
    overlap = overlap_of(bases, arrived_bases, arrival, live, live_partner)
    for sweep_index in range(SWEEPS):
        arrived = lax.all_to_all(
            gather_of(current.astype(jnp.bfloat16), sources), "ia", split_axis=0, concat_axis=0, tiled=True
        )
        update, squares = sweep_of(
            overlap, arrived, arrival, live, weights, shift, virtual, denominators, current, pair_integrals
        )
        squares = jnp.sum(total_of(squares, row_groups, column_groups, sweep_index))
        factor = jnp.minimum(1.0, clip_share * pair_width / jnp.sqrt(squares / total_pairs + 1e-06))
        current = current - factor * update
    return current.reshape(rows_here, columns_here, pair_width, pair_width)


def solution(mesh):
    return jax.shard_map(
        shards,
        mesh=mesh,
        in_specs=(
            P("ia", "ja", None, None),
            P("ia", "ja", None, None),
            P("ia", "ja", None, None),
            P(),
            P(),
            P("ja"),
            P(None, "ja"),
            P(None, "ja", None),
        ),
        out_specs=P("ia", "ja", None, None),
        check_vma=False,
    )
```

```python
import functools

import jax
import jax.numpy as jnp
from jax import lax
from jax.experimental import pallas as pl
from jax.experimental.pallas import tpu as pltpu
from jax.sharding import PartitionSpec as P

BLOCK = 128
NCOUPLE = 4
SWEEPS = 2
MESH = pl.DeviceIdType.MESH


clip_share = 0.4
denominator_floor = 1.0


def rank_within(block_ids):
    entries = block_ids.shape[-1]
    matching = block_ids[..., :, None] == block_ids[..., None, :]
    earlier = jnp.arange(entries)[:, None] > jnp.arange(entries)[None, :]
    return jnp.sum((matching & earlier).astype(jnp.int32), axis=-1)


def total_kernel(n_ia, n_ja, x_ref, o_ref, near, far, near_send, near_recv, far_send, far_recv, own_sem):
    ia, ja = lax.axis_index("ia"), lax.axis_index("ja")
    barrier = pltpu.get_barrier_semaphore()
    for step in range(1, n_ja):
        pl.semaphore_signal(barrier, inc=1, device_id=(ia, lax.rem(ja + step, n_ja)), device_id_type=MESH)
    for step in range(1, n_ia):
        pl.semaphore_signal(barrier, inc=1, device_id=(lax.rem(ia + step, n_ia), ja), device_id_type=MESH)
    own = pltpu.make_async_copy(x_ref, near.at[0], own_sem)
    own.start()
    pl.semaphore_wait(barrier, n_ja + n_ia - 2)
    copies = []
    for step in range(1, n_ja):
        copy = pltpu.make_async_remote_copy(
            src_ref=x_ref,
            dst_ref=near.at[step],
            send_sem=near_send.at[step],
            recv_sem=near_recv.at[step],
            device_id=(ia, lax.rem(ja + step, n_ja)),
            device_id_type=MESH,
        )
        copy.start()
        copies.append(copy)
    own.wait()
    for copy in copies:
        copy.wait()
    copies = []
    for step in range(1, n_ia):
        copy = pltpu.make_async_remote_copy(
            src_ref=near,
            dst_ref=far.at[step - 1],
            send_sem=far_send.at[step],
            recv_sem=far_recv.at[step],
            device_id=(lax.rem(ia + step, n_ia), ja),
            device_id_type=MESH,
        )
        copy.start()
        copies.append(copy)
    for copy in copies:
        copy.wait()
    o_ref[...] = jnp.sum(near[...], axis=0) + jnp.sum(far[...].reshape(((n_ia - 1) * n_ja,) + o_ref.shape), axis=0)


def total_of(x, n_ia, n_ja, call):
    shape = x.shape
    return pl.pallas_call(
        functools.partial(total_kernel, n_ia, n_ja),
        out_shape=jax.ShapeDtypeStruct(shape, jnp.float32),
        in_specs=[pl.BlockSpec(memory_space=pltpu.VMEM)],
        out_specs=pl.BlockSpec(memory_space=pltpu.VMEM),
        scratch_shapes=[
            pltpu.VMEM((n_ja,) + shape, jnp.float32),
            pltpu.VMEM((n_ia - 1, n_ja) + shape, jnp.float32),
            pltpu.SemaphoreType.DMA((n_ja,)),
            pltpu.SemaphoreType.DMA((n_ja,)),
            pltpu.SemaphoreType.DMA((n_ia,)),
            pltpu.SemaphoreType.DMA((n_ia,)),
            pltpu.SemaphoreType.DMA,
        ],
        compiler_params=pltpu.CompilerParams(collective_id=call, has_side_effects=True),
        name="total" + str(call),
    )(x)


def live_rows(shape, live):
    return lax.broadcasted_iota(jnp.int32, shape, 0) < live


def live_columns(shape, live):
    return lax.broadcasted_iota(jnp.int32, shape, 1) < live


def virtual_kernel(live, shift, basis, energy, virtual, denominators):
    p = pl.program_id(0)
    width = basis.shape[2]
    own = basis[0]
    scaled = (own.astype(jnp.float32) * energy[...]).astype(jnp.bfloat16)
    full = jnp.dot(own.T, scaled, preferred_element_type=jnp.float32)
    both = live_rows(full.shape, live[p]) & live_columns(full.shape, live[p])
    full = jnp.where(both, full, 0.0)
    virtual[0] = full.astype(jnp.bfloat16)
    same = lax.broadcasted_iota(jnp.int32, full.shape, 0) == lax.broadcasted_iota(jnp.int32, full.shape, 1)
    picked = jnp.where(same, full, 0.0)
    down = jnp.sum(picked, axis=1, keepdims=True)
    across = jnp.sum(picked, axis=0, keepdims=True)
    denominators[0] = jnp.maximum(down + across - shift[p], denominator_floor)


def virtual_of(basis, energy, live, shift):
    pairs, projected, width = basis.shape
    return pl.pallas_call(
        virtual_kernel,
        out_shape=(
            jax.ShapeDtypeStruct((pairs, width, width), jnp.bfloat16),
            jax.ShapeDtypeStruct((pairs, width, width), jnp.float32),
        ),
        grid_spec=pltpu.PrefetchScalarGridSpec(
            num_scalar_prefetch=2,
            grid=(pairs,),
            in_specs=[
                pl.BlockSpec((1, projected, width), lambda p, *_: (p, 0, 0)),
                pl.BlockSpec((projected, 1), lambda p, *_: (0, 0)),
            ],
            out_specs=[pl.BlockSpec((1, width, width), lambda p, *_: (p, 0, 0))] * 2,
        ),
        cost_estimate=pl.CostEstimate(flops=2 * pairs * projected * width * width, bytes_accessed=4 * pairs * projected * width, transcendentals=0),
    )(live, shift, basis, energy)


def overlap_kernel(valid, pair, index, live, live_partner, own, partner, *rest):
    n = pl.program_id(0)
    out = rest[-1]

    @pl.when(valid[n] > 0)
    def _():
        full = lax.dot_general(own[0], partner[0], (((0,), (0,)), ((), ())), preferred_element_type=jnp.float32)
        both = live_rows(full.shape, live[n]) & live_columns(full.shape, live_partner[n])
        out[0] = jnp.where(both, full, 0.0).astype(jnp.bfloat16)


def overlap_of(tables, place, total, requesters, partners, sofar):
    projected, width = partners.shape[1:]
    valid, pair, index, live, live_partner = tables
    count = valid.shape[0]
    in_specs = [
        pl.BlockSpec((1, projected, width), lambda n, v, p, *_: (p[n], 0, 0)),
        pl.BlockSpec((1, projected, width), lambda n, v, p, k, *_: (k[n], 0, 0)),
    ]
    operands = [valid, pair, index, live, live_partner, requesters, partners]
    aliases = {}
    if sofar is not None:
        in_specs.append(pl.BlockSpec(memory_space=pl.ANY))
        aliases = {len(operands): 0}
        operands.append(sofar)
    return pl.pallas_call(
        overlap_kernel,
        out_shape=jax.ShapeDtypeStruct((total, width, width), jnp.bfloat16),
        grid_spec=pltpu.PrefetchScalarGridSpec(
            num_scalar_prefetch=5,
            grid=(count,),
            in_specs=in_specs,
            out_specs=pl.BlockSpec((1, width, width), lambda n, *_: (place * count + n, 0, 0)),
        ),
        input_output_aliases=aliases,
        cost_estimate=pl.CostEstimate(
            flops=2 * count * projected * width * width, bytes_accessed=4 * count * projected * width, transcendentals=0
        ),
        name="overlap" + str(place),
    )(*operands)


def coupled_kernel(places, slots, who, valid, pair, index, weights, overlap, *rest):
    rounded, out = rest[:places], rest[places]
    total = rest[places + 1] if len(rest) > places + 1 else out
    total[...] = jnp.zeros_like(total)
    for place in range(places):
        for slot in range(slots):
            entry = (place * 2 + who) * slots + slot

            @pl.when(valid[entry] > 0)
            def _(place=place, entry=entry):
                left = overlap[entry]
                first = jnp.dot(left, rounded[place][index[entry]], preferred_element_type=jnp.float32)
                second = lax.dot_general(
                    first.astype(jnp.bfloat16), left, (((1,), (1,)), ((), ())), preferred_element_type=jnp.float32
                )
                total[pair[entry]] += weights[entry] * second

    if total is not out:
        out[...] = total[...].astype(out.dtype)


def coupled_of(who, slots, valid, pair, index, weights, overlap, rounded):
    places = len(rounded)
    shape = rounded[0].shape
    kind = jnp.float32 if who == 0 else jnp.bfloat16
    smem = pl.BlockSpec(memory_space=pltpu.SMEM)
    vmem = pl.BlockSpec(memory_space=pltpu.VMEM)
    return pl.pallas_call(
        functools.partial(coupled_kernel, places, slots, who),
        out_shape=jax.ShapeDtypeStruct(shape, kind),
        in_specs=[smem] * 4 + [vmem] * (1 + places),
        out_specs=vmem,
        scratch_shapes=[pltpu.VMEM(shape, jnp.float32)] if who else [],
        cost_estimate=pl.CostEstimate(
            flops=4 * places * slots * shape[1] ** 3, bytes_accessed=places * 1500000, transcendentals=0
        ),
        name="coupled" + str(who),
    )(valid, pair, index, weights, overlap, *rounded)


def update_kernel(live, shift, own, other, virtual, denominators, current, integrals, update, squares):
    p = pl.program_id(0)
    rounded = current[0].astype(jnp.bfloat16)
    residual = integrals[0] + jnp.dot(virtual[0], rounded, preferred_element_type=jnp.float32)
    residual = residual + jnp.dot(rounded, virtual[0], preferred_element_type=jnp.float32)
    residual = residual - shift[p] * current[0] - (own[0] + other[0].astype(jnp.float32))
    both = live_rows(residual.shape, live[p]) & live_columns(residual.shape, live[p])
    change = jnp.where(both, residual, 0.0) / denominators[0]
    update[0] = change
    squared = change * change
    height, width = squared.shape
    part = jnp.sum(squared.reshape(height // 8, 8, width), axis=0)
    folded = part[:, :128]
    for start in range(128, width, 128):
        folded = folded + part[:, start : start + 128]

    @pl.when(p == 0)
    def _():
        squares[...] = folded

    @pl.when(p > 0)
    def _():
        squares[...] += folded


def update_of(live, shift, own, other, virtual, denominators, current, integrals):
    pairs, width, _ = current.shape
    wide = pl.BlockSpec((1, width, width), lambda p, *_: (p, 0, 0))
    return pl.pallas_call(
        update_kernel,
        out_shape=(
            jax.ShapeDtypeStruct((pairs, width, width), jnp.float32),
            jax.ShapeDtypeStruct((8, 128), jnp.float32),
        ),
        grid_spec=pltpu.PrefetchScalarGridSpec(
            num_scalar_prefetch=2,
            grid=(pairs,),
            in_specs=[wide] * 6,
            out_specs=[wide, pl.BlockSpec((8, 128), lambda p, *_: (0, 0))],
        ),
    )(live, shift, own, other, virtual, denominators, current, integrals)


def along_line(x, groups):
    before, after, found = x, x, [x]
    for _ in range(1, groups // 2):
        before = lax.ppermute(before, "ia", [(i, i + 2) for i in range(groups - 2)])
        after = lax.ppermute(after, "ia", [(i + 2, i) for i in range(groups - 2)])
        found += [before, after]
    return found


def shards(basis, amplitudes, integrals, virt_energy, fock, occ_energy, blocks, couplings):
    rows_here, columns_here, projected, pair_width = basis.shape
    pairs_here = rows_here * columns_here
    requests = NCOUPLE * pairs_here
    row_groups = lax.axis_size("ia")
    column_groups = lax.axis_size("ja")
    slot_count = requests // row_groups
    group_index = lax.axis_index("ia")
    first_row = group_index * rows_here
    total_pairs = rows_here * row_groups * columns_here * column_groups
    live = lax.dynamic_slice_in_dim(blocks, first_row, rows_here, 0).reshape(pairs_here) * BLOCK
    orbital_index = jnp.arange(pair_width, dtype=jnp.int32)
    column_mask = orbital_index[None, :] < live[:, None]
    pair_mask = column_mask[:, :, None] & column_mask[:, None, :]
    twins = [(i, i ^ 1) for i in range(row_groups)]
    groups = [group_index] + [
        group_index + sign * 2 * step for step in range(1, row_groups // 2) for sign in (-1, 1)
    ]
    groups = jnp.stack(groups)
    places = 2 * (row_groups // 2) - 1
    requesters = jnp.stack([group_index, group_index ^ 1])
    asked = couplings.reshape(row_groups, requests)[requesters]
    targets = asked // rows_here
    ranks = rank_within(targets)
    entry = jnp.arange(requests, dtype=jnp.int32)
    entry_pair = jnp.broadcast_to(entry // NCOUPLE, asked.shape)
    entry_column = entry_pair % columns_here
    entry_row = requesters[:, None] * rows_here + entry_pair // columns_here
    chosen = (targets[None, :, None, :] == groups[:, None, None, None]) & (
        ranks[None, :, None, :] == jnp.arange(slot_count, dtype=jnp.int32)[None, None, :, None]
    )

    def listed(values):
        return jnp.sum(jnp.where(chosen, values[None, :, None, :], 0), axis=-1).reshape(-1)

    rows_all = jnp.arange(fock.shape[0], dtype=jnp.int32)
    columns_all = jnp.arange(columns_here, dtype=jnp.int32)
    is_row = entry_row[:, :, None] == rows_all
    is_partner = asked[:, :, None] == rows_all
    is_column = entry_column[:, :, None] == columns_all
    fock_entry = jnp.sum(
        jnp.where(is_row[:, :, :, None] & is_partner[:, :, None, :], fock, 0.0), axis=(2, 3)
    )
    live_entry = BLOCK * jnp.sum(
        jnp.where(is_row[:, :, :, None] & is_column[:, :, None, :], blocks, 0), axis=(2, 3)
    )
    live_other = BLOCK * jnp.sum(
        jnp.where(is_partner[:, :, :, None] & is_column[:, :, None, :], blocks, 0), axis=(2, 3)
    )
    valid = listed(jnp.ones_like(asked))
    pair = listed(entry_pair)
    pair_both = listed(entry_pair + pairs_here * jnp.arange(2, dtype=jnp.int32)[:, None])
    index = listed((asked % rows_here) * columns_here + entry_column)
    weights = listed(fock_entry)
    live_rows_of = listed(live_entry)
    live_columns_of = listed(live_other)
    occupied_diag = lax.dynamic_slice_in_dim(jnp.diagonal(fock), first_row, rows_here, 0)
    shift = (occupied_diag[:, None] + occ_energy[None, :]).reshape(pairs_here)
    bases = basis.reshape(pairs_here, projected, pair_width)
    current = jnp.where(pair_mask, amplitudes.reshape(pairs_here, pair_width, pair_width), 0.0)
    pair_integrals = integrals.reshape(pairs_here, pair_width, pair_width)
    both = jnp.concatenate([bases, lax.ppermute(bases, "ia", twins)])
    line_bases = along_line(bases, row_groups)
    rounded = along_line(current.astype(jnp.bfloat16), row_groups)
    virtual, denominators = virtual_of(bases, virt_energy[:, None], live, shift)
    each = 2 * slot_count
    overlap = None
    for place in range(places):
        here = slice(place * each, (place + 1) * each)
        tables = [x[here] for x in (valid, pair_both, index, live_rows_of, live_columns_of)]
        overlap = overlap_of(tables, place, places * each, both, line_bases[place], overlap)
    for sweep_index in range(SWEEPS):
        if sweep_index:
            rounded = along_line(current.astype(jnp.bfloat16), row_groups)
        lists = (valid, pair, index, weights, overlap, rounded)
        other = lax.ppermute(coupled_of(1, slot_count, *lists), "ia", twins)
        own = coupled_of(0, slot_count, *lists)
        update, squares = update_of(live, shift, own, other, virtual, denominators, current, pair_integrals)
        squares = jnp.sum(total_of(squares, row_groups, column_groups, sweep_index))
        factor = jnp.minimum(1.0, clip_share * pair_width / jnp.sqrt(squares / total_pairs + 1e-06))
        current = current - factor * update
    return current.reshape(rows_here, columns_here, pair_width, pair_width)


def solution(mesh):
    return jax.shard_map(
        shards,
        mesh=mesh,
        in_specs=(
            P("ia", "ja", None, None),
            P("ia", "ja", None, None),
            P("ia", "ja", None, None),
            P(),
            P(),
            P("ja"),
            P(None, "ja"),
            P(None, "ja", None),
        ),
        out_specs=P("ia", "ja", None, None),
        check_vma=False,
    )
```

```python
import functools

import jax
import jax.numpy as jnp
from jax import lax
from jax.experimental import pallas as pl
from jax.experimental.pallas import tpu as pltpu
from jax.sharding import PartitionSpec as P

BLOCK = 128
NCOUPLE = 4
SWEEPS = 2
MESH = pl.DeviceIdType.MESH


clip_share = 0.4
denominator_floor = 1.0


def rank_within(block_ids):
    entries = block_ids.shape[-1]
    matching = block_ids[..., :, None] == block_ids[..., None, :]
    earlier = jnp.arange(entries)[:, None] > jnp.arange(entries)[None, :]
    return jnp.sum((matching & earlier).astype(jnp.int32), axis=-1)


def total_kernel(n_ia, n_ja, x_ref, o_ref, near, far, near_send, near_recv, far_send, far_recv, own_sem):
    ia, ja = lax.axis_index("ia"), lax.axis_index("ja")
    barrier = pltpu.get_barrier_semaphore()
    for step in range(1, n_ja):
        pl.semaphore_signal(barrier, inc=1, device_id=(ia, lax.rem(ja + step, n_ja)), device_id_type=MESH)
    for step in range(1, n_ia):
        pl.semaphore_signal(barrier, inc=1, device_id=(lax.rem(ia + step, n_ia), ja), device_id_type=MESH)
    own = pltpu.make_async_copy(x_ref, near.at[0], own_sem)
    own.start()
    pl.semaphore_wait(barrier, n_ja + n_ia - 2)
    copies = []
    for step in range(1, n_ja):
        copy = pltpu.make_async_remote_copy(
            src_ref=x_ref,
            dst_ref=near.at[step],
            send_sem=near_send.at[step],
            recv_sem=near_recv.at[step],
            device_id=(ia, lax.rem(ja + step, n_ja)),
            device_id_type=MESH,
        )
        copy.start()
        copies.append(copy)
    own.wait()
    for copy in copies:
        copy.wait()
    copies = []
    for step in range(1, n_ia):
        copy = pltpu.make_async_remote_copy(
            src_ref=near,
            dst_ref=far.at[step - 1],
            send_sem=far_send.at[step],
            recv_sem=far_recv.at[step],
            device_id=(lax.rem(ia + step, n_ia), ja),
            device_id_type=MESH,
        )
        copy.start()
        copies.append(copy)
    for copy in copies:
        copy.wait()
    o_ref[...] = jnp.sum(near[...], axis=0) + jnp.sum(far[...].reshape(((n_ia - 1) * n_ja,) + o_ref.shape), axis=0)


def total_of(x, n_ia, n_ja, call):
    shape = x.shape
    return pl.pallas_call(
        functools.partial(total_kernel, n_ia, n_ja),
        out_shape=jax.ShapeDtypeStruct(shape, jnp.float32),
        in_specs=[pl.BlockSpec(memory_space=pltpu.VMEM)],
        out_specs=pl.BlockSpec(memory_space=pltpu.VMEM),
        scratch_shapes=[
            pltpu.VMEM((n_ja,) + shape, jnp.float32),
            pltpu.VMEM((n_ia - 1, n_ja) + shape, jnp.float32),
            pltpu.SemaphoreType.DMA((n_ja,)),
            pltpu.SemaphoreType.DMA((n_ja,)),
            pltpu.SemaphoreType.DMA((n_ia,)),
            pltpu.SemaphoreType.DMA((n_ia,)),
            pltpu.SemaphoreType.DMA,
        ],
        compiler_params=pltpu.CompilerParams(collective_id=call, has_side_effects=True),
        name="total" + str(call),
    )(x)


def live_rows(shape, live):
    return lax.broadcasted_iota(jnp.int32, shape, 0) < live


def live_columns(shape, live):
    return lax.broadcasted_iota(jnp.int32, shape, 1) < live


def virtual_kernel(live, shift, basis, energy, virtual, denominators):
    p = pl.program_id(0)
    width = basis.shape[2]
    own = basis[0]
    scaled = (own.astype(jnp.float32) * energy[...]).astype(jnp.bfloat16)
    full = jnp.dot(own.T, scaled, preferred_element_type=jnp.float32)
    both = live_rows(full.shape, live[p]) & live_columns(full.shape, live[p])
    full = jnp.where(both, full, 0.0)
    virtual[0] = full.astype(jnp.bfloat16)
    same = lax.broadcasted_iota(jnp.int32, full.shape, 0) == lax.broadcasted_iota(jnp.int32, full.shape, 1)
    picked = jnp.where(same, full, 0.0)
    down = jnp.sum(picked, axis=1, keepdims=True)
    across = jnp.sum(picked, axis=0, keepdims=True)
    denominators[0] = jnp.maximum(down + across - shift[p], denominator_floor)


def virtual_of(basis, energy, live, shift):
    pairs, projected, width = basis.shape
    return pl.pallas_call(
        virtual_kernel,
        out_shape=(
            jax.ShapeDtypeStruct((pairs, width, width), jnp.bfloat16),
            jax.ShapeDtypeStruct((pairs, width, width), jnp.float32),
        ),
        grid_spec=pltpu.PrefetchScalarGridSpec(
            num_scalar_prefetch=2,
            grid=(pairs,),
            in_specs=[
                pl.BlockSpec((1, projected, width), lambda p, *_: (p, 0, 0)),
                pl.BlockSpec((projected, 1), lambda p, *_: (0, 0)),
            ],
            out_specs=[pl.BlockSpec((1, width, width), lambda p, *_: (p, 0, 0))] * 2,
        ),
        cost_estimate=pl.CostEstimate(flops=2 * pairs * projected * width * width, bytes_accessed=4 * pairs * projected * width, transcendentals=0),
    )(live, shift, basis, energy)


def overlap_kernel(base, half, valid, pair, index, live, live_partner, own, twin, partner, *rest):
    n = pl.program_id(0)
    out = rest[-1]
    entry = base + n

    def product(mine):
        full = lax.dot_general(mine[0], partner[0], (((0,), (0,)), ((), ())), preferred_element_type=jnp.float32)
        both = live_rows(full.shape, live[entry]) & live_columns(full.shape, live_partner[entry])
        out[0] = jnp.where(both, full, 0.0).astype(jnp.bfloat16)

    @pl.when((valid[entry] > 0) & (n < half))
    def _():
        product(own)

    @pl.when((valid[entry] > 0) & (n >= half))
    def _():
        product(twin)


def overlap_of(tables, place, count, total, offset, own, twin, partners, sofar):
    projected, width = partners.shape[1:]
    half = count // 2
    base = place * count
    in_specs = [
        pl.BlockSpec((1, projected, width), lambda n, v, p, *_: (p[base + jnp.minimum(n, half - 1)], 0, 0)),
        pl.BlockSpec((1, projected, width), lambda n, v, p, *_: (p[base + jnp.maximum(n, half)], 0, 0)),
        pl.BlockSpec((1, projected, width), lambda n, v, p, k, *_: (k[base + n], 0, 0)),
    ]
    operands = [*tables, own, twin, partners]
    aliases = {}
    if sofar is not None:
        in_specs.append(pl.BlockSpec(memory_space=pl.ANY))
        aliases = {len(operands): 0}
        operands.append(sofar)
    return pl.pallas_call(
        functools.partial(overlap_kernel, base, half),
        out_shape=jax.ShapeDtypeStruct((total, width, width), jnp.bfloat16),
        grid_spec=pltpu.PrefetchScalarGridSpec(
            num_scalar_prefetch=5,
            grid=(count,),
            in_specs=in_specs,
            out_specs=pl.BlockSpec((1, width, width), lambda n, *_: (offset + n, 0, 0)),
        ),
        input_output_aliases=aliases,
        cost_estimate=pl.CostEstimate(
            flops=2 * count * projected * width * width, bytes_accessed=4 * count * projected * width, transcendentals=0
        ),
        name="overlap" + str(place),
    )(*operands)


def coupled_kernel(places, slots, who, valid, pair, index, weights, overlap, far_before, far_after, *rest):
    rounded, out = rest[:places], rest[places]
    total = rest[places + 1] if len(rest) > places + 1 else out
    total[...] = jnp.zeros_like(total)
    for place in range(places):
        for slot in range(slots):
            within = who * slots + slot
            entry = place * 2 * slots + within

            @pl.when(valid[entry] > 0)
            def _(place=place, entry=entry, within=within):
                if place == places - 2:
                    left = far_before[within]
                elif place == places - 1:
                    left = far_after[within]
                else:
                    left = overlap[entry]
                first = jnp.dot(left, rounded[place][index[entry]], preferred_element_type=jnp.float32)
                second = lax.dot_general(
                    first.astype(jnp.bfloat16), left, (((1,), (1,)), ((), ())), preferred_element_type=jnp.float32
                )
                total[pair[entry]] += weights[entry] * second

    if total is not out:
        out[...] = total[...].astype(out.dtype)


def coupled_of(who, slots, valid, pair, index, weights, overlaps, rounded):
    places = len(rounded)
    shape = rounded[0].shape
    kind = jnp.float32 if who == 0 else jnp.bfloat16
    smem = pl.BlockSpec(memory_space=pltpu.SMEM)
    vmem = pl.BlockSpec(memory_space=pltpu.VMEM)
    return pl.pallas_call(
        functools.partial(coupled_kernel, places, slots, who),
        out_shape=jax.ShapeDtypeStruct(shape, kind),
        in_specs=[smem] * 4 + [vmem] * (3 + places),
        out_specs=vmem,
        scratch_shapes=[pltpu.VMEM(shape, jnp.float32)] if who else [],
        cost_estimate=pl.CostEstimate(
            flops=4 * places * slots * shape[1] ** 3, bytes_accessed=places * 1500000, transcendentals=0
        ),
        name="coupled" + str(who),
    )(valid, pair, index, weights, *overlaps, *rounded)


def update_kernel(live, shift, own, other, virtual, denominators, current, integrals, update, squares):
    p = pl.program_id(0)
    rounded = current[0].astype(jnp.bfloat16)
    residual = integrals[0] + jnp.dot(virtual[0], rounded, preferred_element_type=jnp.float32)
    residual = residual + jnp.dot(rounded, virtual[0], preferred_element_type=jnp.float32)
    residual = residual - shift[p] * current[0] - (own[0] + other[0].astype(jnp.float32))
    both = live_rows(residual.shape, live[p]) & live_columns(residual.shape, live[p])
    change = jnp.where(both, residual, 0.0) / denominators[0]
    update[0] = change
    squared = change * change
    height, width = squared.shape
    part = jnp.sum(squared.reshape(height // 8, 8, width), axis=0)
    folded = part[:, :128]
    for start in range(128, width, 128):
        folded = folded + part[:, start : start + 128]

    @pl.when(p == 0)
    def _():
        squares[...] = folded

    @pl.when(p > 0)
    def _():
        squares[...] += folded


def update_of(live, shift, own, other, virtual, denominators, current, integrals):
    pairs, width, _ = current.shape
    wide = pl.BlockSpec((1, width, width), lambda p, *_: (p, 0, 0))
    return pl.pallas_call(
        update_kernel,
        out_shape=(
            jax.ShapeDtypeStruct((pairs, width, width), jnp.float32),
            jax.ShapeDtypeStruct((8, 128), jnp.float32),
        ),
        grid_spec=pltpu.PrefetchScalarGridSpec(
            num_scalar_prefetch=2,
            grid=(pairs,),
            in_specs=[wide] * 6,
            out_specs=[wide, pl.BlockSpec((8, 128), lambda p, *_: (0, 0))],
        ),
    )(live, shift, own, other, virtual, denominators, current, integrals)


def onward(x, groups):
    return lax.ppermute(x, "ia", [(i, i + 2) for i in range(groups - 2)])


def backward(x, groups):
    return lax.ppermute(x, "ia", [(i + 2, i) for i in range(groups - 2)])


def along_line(x, groups):
    before, after, found = x, x, [x]
    for _ in range(1, groups // 2):
        before, after = onward(before, groups), backward(after, groups)
        found += [before, after]
    return found


def shards(basis, amplitudes, integrals, virt_energy, fock, occ_energy, blocks, couplings):
    rows_here, columns_here, projected, pair_width = basis.shape
    pairs_here = rows_here * columns_here
    requests = NCOUPLE * pairs_here
    row_groups = lax.axis_size("ia")
    column_groups = lax.axis_size("ja")
    slot_count = requests // row_groups
    group_index = lax.axis_index("ia")
    first_row = group_index * rows_here
    total_pairs = rows_here * row_groups * columns_here * column_groups
    live = lax.dynamic_slice_in_dim(blocks, first_row, rows_here, 0).reshape(pairs_here) * BLOCK
    orbital_index = jnp.arange(pair_width, dtype=jnp.int32)
    column_mask = orbital_index[None, :] < live[:, None]
    pair_mask = column_mask[:, :, None] & column_mask[:, None, :]
    twins = [(i, i ^ 1) for i in range(row_groups)]
    last = row_groups // 2 - 1
    seen = [(group_index, group_index)] + [
        (group_index, group_index + sign * 2 * step) for step in range(1, last + 1) for sign in (-1, 1)
    ]
    places = len(seen)
    seen.append((group_index + 2, group_index - 2 * (last - 1)))
    seen.append((group_index - 2, group_index + 2 * (last - 1)))
    groups = jnp.stack([group for _, group in seen])
    requesters = jnp.stack([asking for asking, _ in seen])
    exists = (requesters >= 0) & (requesters < row_groups)
    requesters = jnp.clip(requesters, 0, row_groups - 1)
    requesters = jnp.stack([requesters, requesters ^ 1], axis=1)
    asked = couplings.reshape(row_groups, requests)[requesters]
    targets = asked // rows_here
    ranks = rank_within(targets)
    entry = jnp.arange(requests, dtype=jnp.int32)
    entry_pair = jnp.broadcast_to(entry // NCOUPLE, asked.shape)
    entry_column = entry_pair % columns_here
    entry_row = requesters[:, :, None] * rows_here + entry_pair // columns_here
    chosen = (
        (targets[:, :, None, :] == groups[:, None, None, None])
        & (ranks[:, :, None, :] == jnp.arange(slot_count, dtype=jnp.int32)[None, None, :, None])
        & exists[:, None, None, None]
    )

    def listed(values):
        return jnp.sum(jnp.where(chosen, values[:, :, None, :], 0), axis=-1).reshape(-1)

    rows_all = jnp.arange(fock.shape[0], dtype=jnp.int32)
    columns_all = jnp.arange(columns_here, dtype=jnp.int32)
    is_row = entry_row[..., None] == rows_all
    is_partner = asked[..., None] == rows_all
    is_column = entry_column[..., None] == columns_all
    fock_entry = jnp.sum(
        jnp.where(is_row[..., :, None] & is_partner[..., None, :], fock, 0.0), axis=(-2, -1)
    )
    live_entry = BLOCK * jnp.sum(
        jnp.where(is_row[..., :, None] & is_column[..., None, :], blocks, 0), axis=(-2, -1)
    )
    live_other = BLOCK * jnp.sum(
        jnp.where(is_partner[..., :, None] & is_column[..., None, :], blocks, 0), axis=(-2, -1)
    )
    valid = listed(jnp.ones_like(asked))
    pair = listed(entry_pair)
    index = listed((asked % rows_here) * columns_here + entry_column)
    weights = listed(fock_entry)
    live_rows_of = listed(live_entry)
    live_columns_of = listed(live_other)
    occupied_diag = lax.dynamic_slice_in_dim(jnp.diagonal(fock), first_row, rows_here, 0)
    shift = (occupied_diag[:, None] + occ_energy[None, :]).reshape(pairs_here)
    bases = basis.reshape(pairs_here, projected, pair_width)
    current = jnp.where(pair_mask, amplitudes.reshape(pairs_here, pair_width, pair_width), 0.0)
    pair_integrals = integrals.reshape(pairs_here, pair_width, pair_width)
    each = 2 * slot_count
    direct = places - 2
    tables = (valid, pair, index, live_rows_of, live_columns_of)
    twin = lax.ppermute(bases, "ia", twins)
    line_bases, before, after = [bases], bases, bases
    overlap, twin_before, twin_after, done = None, None, None, 0
    virtual, denominators = virtual_of(bases, virt_energy[:, None], live, shift)
    for step in range(1, last):
        before, after = onward(before, row_groups), backward(after, row_groups)
        if step > 1:
            while done < 2 * step - 1:
                overlap = overlap_of(
                    tables, done, each, direct * each, done * each, bases, twin, line_bases[done], overlap
                )
                done += 1
            before, after, overlap = lax.optimization_barrier((before, after, overlap))
        if step == 1:
            twin_before, twin_after = lax.ppermute(before, "ia", twins), lax.ppermute(after, "ia", twins)
        line_bases += [before, after]
    rounded = along_line(current.astype(jnp.bfloat16), row_groups)
    far_before = overlap_of(tables, places, each, each, 0, line_bases[2], twin_after, before, None)
    far_after = overlap_of(tables, places + 1, each, each, 0, line_bases[1], twin_before, after, None)
    far_before, far_after, overlap = lax.optimization_barrier((far_before, far_after, overlap))
    far_before, far_after = onward(far_before, row_groups), backward(far_after, row_groups)
    while done < direct:
        overlap = overlap_of(tables, done, each, direct * each, done * each, bases, twin, line_bases[done], overlap)
        done += 1
    overlaps = (overlap, far_before, far_after)
    for sweep_index in range(SWEEPS):
        if sweep_index:
            rounded = along_line(current.astype(jnp.bfloat16), row_groups)
        lists = (valid, pair, index, weights, overlaps, rounded)
        other = lax.ppermute(coupled_of(1, slot_count, *lists), "ia", twins)
        own = coupled_of(0, slot_count, *lists)
        update, squares = update_of(live, shift, own, other, virtual, denominators, current, pair_integrals)
        squares = jnp.sum(total_of(squares, row_groups, column_groups, sweep_index))
        factor = jnp.minimum(1.0, clip_share * pair_width / jnp.sqrt(squares / total_pairs + 1e-06))
        current = current - factor * update
    return current.reshape(rows_here, columns_here, pair_width, pair_width)


def solution(mesh):
    return jax.shard_map(
        shards,
        mesh=mesh,
        in_specs=(
            P("ia", "ja", None, None),
            P("ia", "ja", None, None),
            P("ia", "ja", None, None),
            P(),
            P(),
            P("ja"),
            P(None, "ja"),
            P(None, "ja", None),
        ),
        out_specs=P("ia", "ja", None, None),
        check_vma=False,
    )
```

```python
import functools

import jax
import jax.numpy as jnp
from jax import lax
from jax.experimental import pallas as pl
from jax.experimental.pallas import tpu as pltpu
from jax.sharding import PartitionSpec as P

BLOCK = 128
NCOUPLE = 4
SWEEPS = 2
MESH = pl.DeviceIdType.MESH


clip_share = 0.4
denominator_floor = 1.0


def rank_within(block_ids):
    entries = block_ids.shape[-1]
    matching = block_ids[..., :, None] == block_ids[..., None, :]
    earlier = jnp.arange(entries)[:, None] > jnp.arange(entries)[None, :]
    return jnp.sum((matching & earlier).astype(jnp.int32), axis=-1)


def total_kernel(n_ia, n_ja, x_ref, o_ref, near, far, near_send, near_recv, far_send, far_recv, own_sem):
    ia, ja = lax.axis_index("ia"), lax.axis_index("ja")
    barrier = pltpu.get_barrier_semaphore()
    for step in range(1, n_ja):
        pl.semaphore_signal(barrier, inc=1, device_id=(ia, lax.rem(ja + step, n_ja)), device_id_type=MESH)
    for step in range(1, n_ia):
        pl.semaphore_signal(barrier, inc=1, device_id=(lax.rem(ia + step, n_ia), ja), device_id_type=MESH)
    own = pltpu.make_async_copy(x_ref, near.at[0], own_sem)
    own.start()
    pl.semaphore_wait(barrier, n_ja + n_ia - 2)
    copies = []
    for step in range(1, n_ja):
        copy = pltpu.make_async_remote_copy(
            src_ref=x_ref,
            dst_ref=near.at[step],
            send_sem=near_send.at[step],
            recv_sem=near_recv.at[step],
            device_id=(ia, lax.rem(ja + step, n_ja)),
            device_id_type=MESH,
        )
        copy.start()
        copies.append(copy)
    own.wait()
    for copy in copies:
        copy.wait()
    copies = []
    for step in range(1, n_ia):
        copy = pltpu.make_async_remote_copy(
            src_ref=near,
            dst_ref=far.at[step - 1],
            send_sem=far_send.at[step],
            recv_sem=far_recv.at[step],
            device_id=(lax.rem(ia + step, n_ia), ja),
            device_id_type=MESH,
        )
        copy.start()
        copies.append(copy)
    for copy in copies:
        copy.wait()
    o_ref[...] = jnp.sum(near[...], axis=0) + jnp.sum(far[...].reshape(((n_ia - 1) * n_ja,) + o_ref.shape), axis=0)


def total_of(x, n_ia, n_ja, call):
    shape = x.shape
    return pl.pallas_call(
        functools.partial(total_kernel, n_ia, n_ja),
        out_shape=jax.ShapeDtypeStruct(shape, jnp.float32),
        in_specs=[pl.BlockSpec(memory_space=pltpu.VMEM)],
        out_specs=pl.BlockSpec(memory_space=pltpu.VMEM),
        scratch_shapes=[
            pltpu.VMEM((n_ja,) + shape, jnp.float32),
            pltpu.VMEM((n_ia - 1, n_ja) + shape, jnp.float32),
            pltpu.SemaphoreType.DMA((n_ja,)),
            pltpu.SemaphoreType.DMA((n_ja,)),
            pltpu.SemaphoreType.DMA((n_ia,)),
            pltpu.SemaphoreType.DMA((n_ia,)),
            pltpu.SemaphoreType.DMA,
        ],
        compiler_params=pltpu.CompilerParams(collective_id=call, has_side_effects=True),
        name="total" + str(call),
    )(x)


def live_rows(shape, live):
    return lax.broadcasted_iota(jnp.int32, shape, 0) < live


def live_columns(shape, live):
    return lax.broadcasted_iota(jnp.int32, shape, 1) < live


def virtual_kernel(live, shift, basis, energy, virtual, denominators):
    p = pl.program_id(0)
    width = basis.shape[2]
    own = basis[0]
    scaled = (own.astype(jnp.float32) * energy[...]).astype(jnp.bfloat16)
    full = jnp.dot(own.T, scaled, preferred_element_type=jnp.float32)
    both = live_rows(full.shape, live[p]) & live_columns(full.shape, live[p])
    full = jnp.where(both, full, 0.0)
    virtual[0] = full.astype(jnp.bfloat16)
    same = lax.broadcasted_iota(jnp.int32, full.shape, 0) == lax.broadcasted_iota(jnp.int32, full.shape, 1)
    picked = jnp.where(same, full, 0.0)
    down = jnp.sum(picked, axis=1, keepdims=True)
    across = jnp.sum(picked, axis=0, keepdims=True)
    denominators[0] = jnp.maximum(down + across - shift[p], denominator_floor)


def virtual_of(basis, energy, live, shift):
    pairs, projected, width = basis.shape
    return pl.pallas_call(
        virtual_kernel,
        out_shape=(
            jax.ShapeDtypeStruct((pairs, width, width), jnp.bfloat16),
            jax.ShapeDtypeStruct((pairs, width, width), jnp.float32),
        ),
        grid_spec=pltpu.PrefetchScalarGridSpec(
            num_scalar_prefetch=2,
            grid=(pairs,),
            in_specs=[
                pl.BlockSpec((1, projected, width), lambda p, *_: (p, 0, 0)),
                pl.BlockSpec((projected, 1), lambda p, *_: (0, 0)),
            ],
            out_specs=[pl.BlockSpec((1, width, width), lambda p, *_: (p, 0, 0))] * 2,
        ),
        cost_estimate=pl.CostEstimate(flops=2 * pairs * projected * width * width, bytes_accessed=4 * pairs * projected * width, transcendentals=0),
    )(live, shift, basis, energy)


def overlap_kernel(base, half, valid, pair, index, live, live_partner, own, twin, partner, *rest):
    n = pl.program_id(0)
    out = rest[-1]
    entry = base + n

    def product(mine):
        full = lax.dot_general(mine[0], partner[0], (((0,), (0,)), ((), ())), preferred_element_type=jnp.float32)
        both = live_rows(full.shape, live[entry]) & live_columns(full.shape, live_partner[entry])
        out[0] = jnp.where(both, full, 0.0).astype(jnp.bfloat16)

    @pl.when((valid[entry] > 0) & (n < half))
    def _():
        product(own)

    @pl.when((valid[entry] > 0) & (n >= half))
    def _():
        product(twin)


def overlap_of(tables, place, count, total, offset, own, twin, partners, sofar):
    projected, width = partners.shape[1:]
    half = count // 2
    base = place * count
    in_specs = [
        pl.BlockSpec((1, projected, width), lambda n, v, p, *_: (p[base + jnp.minimum(n, half - 1)], 0, 0)),
        pl.BlockSpec((1, projected, width), lambda n, v, p, *_: (p[base + jnp.maximum(n, half)], 0, 0)),
        pl.BlockSpec((1, projected, width), lambda n, v, p, k, *_: (k[base + n], 0, 0)),
    ]
    operands = [*tables, own, twin, partners]
    aliases = {}
    if sofar is not None:
        in_specs.append(pl.BlockSpec(memory_space=pl.ANY))
        aliases = {len(operands): 0}
        operands.append(sofar)
    return pl.pallas_call(
        functools.partial(overlap_kernel, base, half),
        out_shape=jax.ShapeDtypeStruct((total, width, width), jnp.bfloat16),
        grid_spec=pltpu.PrefetchScalarGridSpec(
            num_scalar_prefetch=5,
            grid=(count,),
            in_specs=in_specs,
            out_specs=pl.BlockSpec((1, width, width), lambda n, *_: (offset + n, 0, 0)),
        ),
        input_output_aliases=aliases,
        cost_estimate=pl.CostEstimate(
            flops=2 * count * projected * width * width, bytes_accessed=4 * count * projected * width, transcendentals=0
        ),
        name="overlap" + str(place),
    )(*operands)


def coupled_kernel(places, slots, who, valid, pair, index, weights, overlap, far_before, far_after, *rest):
    rounded, out = rest[:places], rest[places]
    total = rest[places + 1] if len(rest) > places + 1 else out
    total[...] = jnp.zeros_like(total)
    for place in range(places):
        for slot in range(slots):
            within = who * slots + slot
            entry = place * 2 * slots + within

            @pl.when(valid[entry] > 0)
            def _(place=place, entry=entry, within=within):
                if place == places - 2:
                    left = far_before[within]
                elif place == places - 1:
                    left = far_after[within]
                else:
                    left = overlap[entry]
                first = jnp.dot(left, rounded[place][index[entry]], preferred_element_type=jnp.float32)
                second = lax.dot_general(
                    first.astype(jnp.bfloat16), left, (((1,), (1,)), ((), ())), preferred_element_type=jnp.float32
                )
                total[pair[entry]] += weights[entry] * second

    if total is not out:
        out[...] = total[...].astype(out.dtype)


def coupled_of(who, slots, valid, pair, index, weights, overlaps, rounded):
    places = len(rounded)
    shape = rounded[0].shape
    kind = jnp.float32 if who == 0 else jnp.bfloat16
    smem = pl.BlockSpec(memory_space=pltpu.SMEM)
    vmem = pl.BlockSpec(memory_space=pltpu.VMEM)
    return pl.pallas_call(
        functools.partial(coupled_kernel, places, slots, who),
        out_shape=jax.ShapeDtypeStruct(shape, kind),
        in_specs=[smem] * 4 + [vmem] * (3 + places),
        out_specs=vmem,
        scratch_shapes=[pltpu.VMEM(shape, jnp.float32)] if who else [],
        cost_estimate=pl.CostEstimate(
            flops=4 * places * slots * shape[1] ** 3, bytes_accessed=places * 1500000, transcendentals=0
        ),
        name="coupled" + str(who),
    )(valid, pair, index, weights, *overlaps, *rounded)


def update_kernel(live, shift, own, other, virtual, denominators, current, integrals, update, squares):
    p = pl.program_id(0)
    rounded = current[0].astype(jnp.bfloat16)
    residual = integrals[0] + jnp.dot(virtual[0], rounded, preferred_element_type=jnp.float32)
    residual = residual + jnp.dot(rounded, virtual[0], preferred_element_type=jnp.float32)
    residual = residual - shift[p] * current[0] - (own[0] + other[0].astype(jnp.float32))
    both = live_rows(residual.shape, live[p]) & live_columns(residual.shape, live[p])
    change = jnp.where(both, residual, 0.0) / denominators[0]
    update[0] = change
    squared = change * change
    height, width = squared.shape
    part = jnp.sum(squared.reshape(height // 8, 8, width), axis=0)
    folded = part[:, :128]
    for start in range(128, width, 128):
        folded = folded + part[:, start : start + 128]

    @pl.when(p == 0)
    def _():
        squares[...] = folded

    @pl.when(p > 0)
    def _():
        squares[...] += folded


def update_of(live, shift, own, other, virtual, denominators, current, integrals):
    pairs, width, _ = current.shape
    wide = pl.BlockSpec((1, width, width), lambda p, *_: (p, 0, 0))
    return pl.pallas_call(
        update_kernel,
        out_shape=(
            jax.ShapeDtypeStruct((pairs, width, width), jnp.float32),
            jax.ShapeDtypeStruct((8, 128), jnp.float32),
        ),
        grid_spec=pltpu.PrefetchScalarGridSpec(
            num_scalar_prefetch=2,
            grid=(pairs,),
            in_specs=[wide] * 6,
            out_specs=[wide, pl.BlockSpec((8, 128), lambda p, *_: (0, 0))],
        ),
    )(live, shift, own, other, virtual, denominators, current, integrals)


def onward(x, groups):
    return lax.ppermute(x, "ia", [(i, i + 2) for i in range(groups - 2)])


def backward(x, groups):
    return lax.ppermute(x, "ia", [(i + 2, i) for i in range(groups - 2)])


def along_line(x, groups):
    before, after, found = x, x, [x]
    for _ in range(1, groups // 2):
        before, after = onward(before, groups), backward(after, groups)
        found += [before, after]
    return found


def shards(basis, amplitudes, integrals, virt_energy, fock, occ_energy, blocks, couplings):
    rows_here, columns_here, projected, pair_width = basis.shape
    pairs_here = rows_here * columns_here
    requests = NCOUPLE * pairs_here
    row_groups = lax.axis_size("ia")
    column_groups = lax.axis_size("ja")
    slot_count = requests // row_groups
    group_index = lax.axis_index("ia")
    first_row = group_index * rows_here
    total_pairs = rows_here * row_groups * columns_here * column_groups
    live = lax.dynamic_slice_in_dim(blocks, first_row, rows_here, 0).reshape(pairs_here) * BLOCK
    orbital_index = jnp.arange(pair_width, dtype=jnp.int32)
    column_mask = orbital_index[None, :] < live[:, None]
    pair_mask = column_mask[:, :, None] & column_mask[:, None, :]
    twins = [(i, i ^ 1) for i in range(row_groups)]
    last = row_groups // 2 - 1
    seen = [(group_index, group_index)] + [
        (group_index, group_index + sign * 2 * step) for step in range(1, last + 1) for sign in (-1, 1)
    ]
    places = len(seen)
    seen.append((group_index + 2, group_index - 2 * (last - 1)))
    seen.append((group_index - 2, group_index + 2 * (last - 1)))
    groups = jnp.stack([group for _, group in seen])
    requesters = jnp.stack([asking for asking, _ in seen])
    exists = (requesters >= 0) & (requesters < row_groups)
    requesters = jnp.clip(requesters, 0, row_groups - 1)
    requesters = jnp.stack([requesters, requesters ^ 1], axis=1)
    asked = couplings.reshape(row_groups, requests)[requesters]
    targets = asked // rows_here
    ranks = rank_within(targets)
    entry = jnp.arange(requests, dtype=jnp.int32)
    entry_pair = jnp.broadcast_to(entry // NCOUPLE, asked.shape)
    entry_column = entry_pair % columns_here
    entry_row = requesters[:, :, None] * rows_here + entry_pair // columns_here
    chosen = (
        (targets[:, :, None, :] == groups[:, None, None, None])
        & (ranks[:, :, None, :] == jnp.arange(slot_count, dtype=jnp.int32)[None, None, :, None])
        & exists[:, None, None, None]
    )

    def listed(values):
        return jnp.sum(jnp.where(chosen, values[:, :, None, :], 0), axis=-1).reshape(-1)

    rows_all = jnp.arange(fock.shape[0], dtype=jnp.int32)
    columns_all = jnp.arange(columns_here, dtype=jnp.int32)
    is_row = entry_row[..., None] == rows_all
    is_partner = asked[..., None] == rows_all
    is_column = entry_column[..., None] == columns_all
    fock_entry = jnp.sum(
        jnp.where(is_row[..., :, None] & is_partner[..., None, :], fock, 0.0), axis=(-2, -1)
    )
    live_entry = BLOCK * jnp.sum(
        jnp.where(is_row[..., :, None] & is_column[..., None, :], blocks, 0), axis=(-2, -1)
    )
    live_other = BLOCK * jnp.sum(
        jnp.where(is_partner[..., :, None] & is_column[..., None, :], blocks, 0), axis=(-2, -1)
    )
    valid = listed(jnp.ones_like(asked))
    pair = listed(entry_pair)
    index = listed((asked % rows_here) * columns_here + entry_column)
    weights = listed(fock_entry)
    live_rows_of = listed(live_entry)
    live_columns_of = listed(live_other)
    occupied_diag = lax.dynamic_slice_in_dim(jnp.diagonal(fock), first_row, rows_here, 0)
    shift = (occupied_diag[:, None] + occ_energy[None, :]).reshape(pairs_here)
    bases = basis.reshape(pairs_here, projected, pair_width)
    current = jnp.where(pair_mask, amplitudes.reshape(pairs_here, pair_width, pair_width), 0.0)
    pair_integrals = integrals.reshape(pairs_here, pair_width, pair_width)
    each = 2 * slot_count
    direct = places - 2
    tables = (valid, pair, index, live_rows_of, live_columns_of)
    twin = lax.ppermute(bases, "ia", twins)
    line_bases, before, after = [bases], bases, bases
    rounded = [current.astype(jnp.bfloat16)]
    earlier, later = onward(rounded[0], row_groups), backward(rounded[0], row_groups)
    rounded += [earlier, later]
    overlap, twin_before, twin_after, done = None, None, None, 0
    virtual, denominators = virtual_of(bases, virt_energy[:, None], live, shift)
    for step in range(1, last):
        before, after = onward(before, row_groups), backward(after, row_groups)
        if step > 1:
            while done < 2 * step - 1:
                overlap = overlap_of(
                    tables, done, each, direct * each, done * each, bases, twin, line_bases[done], overlap
                )
                done += 1
            earlier, later, overlap = lax.optimization_barrier((earlier, later, overlap))
            earlier, later = onward(earlier, row_groups), backward(later, row_groups)
            rounded += [earlier, later]
            before, after, overlap = lax.optimization_barrier((before, after, overlap))
        if step == 1:
            twin_before, twin_after = lax.ppermute(before, "ia", twins), lax.ppermute(after, "ia", twins)
        line_bases += [before, after]
    far_before = overlap_of(tables, places, each, each, 0, line_bases[2], twin_after, before, None)
    far_after = overlap_of(tables, places + 1, each, each, 0, line_bases[1], twin_before, after, None)
    far_before, far_after, overlap = lax.optimization_barrier((far_before, far_after, overlap))
    far_before, far_after = onward(far_before, row_groups), backward(far_after, row_groups)
    rounded += [onward(earlier, row_groups), backward(later, row_groups)]
    while done < direct:
        overlap = overlap_of(tables, done, each, direct * each, done * each, bases, twin, line_bases[done], overlap)
        done += 1
    overlaps = (overlap, far_before, far_after)
    for sweep_index in range(SWEEPS):
        if sweep_index:
            rounded = along_line(current.astype(jnp.bfloat16), row_groups)
        lists = (valid, pair, index, weights, overlaps, rounded)
        other = lax.ppermute(coupled_of(1, slot_count, *lists), "ia", twins)
        own = coupled_of(0, slot_count, *lists)
        update, squares = update_of(live, shift, own, other, virtual, denominators, current, pair_integrals)
        squares = jnp.sum(total_of(squares, row_groups, column_groups, sweep_index))
        factor = jnp.minimum(1.0, clip_share * pair_width / jnp.sqrt(squares / total_pairs + 1e-06))
        current = current - factor * update
    return current.reshape(rows_here, columns_here, pair_width, pair_width)


def solution(mesh):
    return jax.shard_map(
        shards,
        mesh=mesh,
        in_specs=(
            P("ia", "ja", None, None),
            P("ia", "ja", None, None),
            P("ia", "ja", None, None),
            P(),
            P(),
            P("ja"),
            P(None, "ja"),
            P(None, "ja", None),
        ),
        out_specs=P("ia", "ja", None, None),
        check_vma=False,
    )
```

```python
import functools

import jax
import jax.numpy as jnp
from jax import lax
from jax.experimental import pallas as pl
from jax.experimental.pallas import tpu as pltpu
from jax.sharding import PartitionSpec as P

BLOCK = 128
NCOUPLE = 4
SWEEPS = 2
MESH = pl.DeviceIdType.MESH


clip_share = 0.4
denominator_floor = 1.0


def rank_within(block_ids):
    entries = block_ids.shape[-1]
    matching = block_ids[..., :, None] == block_ids[..., None, :]
    earlier = jnp.arange(entries)[:, None] > jnp.arange(entries)[None, :]
    return jnp.sum((matching & earlier).astype(jnp.int32), axis=-1)


def total_kernel(n_ia, n_ja, x_ref, o_ref, near, far, near_send, near_recv, far_send, far_recv, own_sem):
    ia, ja = lax.axis_index("ia"), lax.axis_index("ja")
    barrier = pltpu.get_barrier_semaphore()
    for step in range(1, n_ja):
        pl.semaphore_signal(barrier, inc=1, device_id=(ia, lax.rem(ja + step, n_ja)), device_id_type=MESH)
    for step in range(1, n_ia):
        pl.semaphore_signal(barrier, inc=1, device_id=(lax.rem(ia + step, n_ia), ja), device_id_type=MESH)
    own = pltpu.make_async_copy(x_ref, near.at[0], own_sem)
    own.start()
    pl.semaphore_wait(barrier, n_ja + n_ia - 2)
    copies = []
    for step in range(1, n_ja):
        copy = pltpu.make_async_remote_copy(
            src_ref=x_ref,
            dst_ref=near.at[step],
            send_sem=near_send.at[step],
            recv_sem=near_recv.at[step],
            device_id=(ia, lax.rem(ja + step, n_ja)),
            device_id_type=MESH,
        )
        copy.start()
        copies.append(copy)
    own.wait()
    for copy in copies:
        copy.wait()
    copies = []
    for step in range(1, n_ia):
        copy = pltpu.make_async_remote_copy(
            src_ref=near,
            dst_ref=far.at[step - 1],
            send_sem=far_send.at[step],
            recv_sem=far_recv.at[step],
            device_id=(lax.rem(ia + step, n_ia), ja),
            device_id_type=MESH,
        )
        copy.start()
        copies.append(copy)
    for copy in copies:
        copy.wait()
    o_ref[...] = jnp.sum(near[...], axis=0) + jnp.sum(far[...].reshape(((n_ia - 1) * n_ja,) + o_ref.shape), axis=0)


def total_of(x, n_ia, n_ja, call):
    shape = x.shape
    return pl.pallas_call(
        functools.partial(total_kernel, n_ia, n_ja),
        out_shape=jax.ShapeDtypeStruct(shape, jnp.float32),
        in_specs=[pl.BlockSpec(memory_space=pltpu.VMEM)],
        out_specs=pl.BlockSpec(memory_space=pltpu.VMEM),
        scratch_shapes=[
            pltpu.VMEM((n_ja,) + shape, jnp.float32),
            pltpu.VMEM((n_ia - 1, n_ja) + shape, jnp.float32),
            pltpu.SemaphoreType.DMA((n_ja,)),
            pltpu.SemaphoreType.DMA((n_ja,)),
            pltpu.SemaphoreType.DMA((n_ia,)),
            pltpu.SemaphoreType.DMA((n_ia,)),
            pltpu.SemaphoreType.DMA,
        ],
        compiler_params=pltpu.CompilerParams(collective_id=call, has_side_effects=True),
        name="total" + str(call),
    )(x)


def live_rows(shape, live):
    return lax.broadcasted_iota(jnp.int32, shape, 0) < live


def live_columns(shape, live):
    return lax.broadcasted_iota(jnp.int32, shape, 1) < live


def virtual_kernel(live, shift, basis, energy, virtual, denominators):
    p = pl.program_id(0)
    width = basis.shape[2]
    own = basis[0]
    scaled = (own.astype(jnp.float32) * energy[...]).astype(jnp.bfloat16)
    full = jnp.dot(own.T, scaled, preferred_element_type=jnp.float32)
    both = live_rows(full.shape, live[p]) & live_columns(full.shape, live[p])
    full = jnp.where(both, full, 0.0)
    virtual[0] = full.astype(jnp.bfloat16)
    same = lax.broadcasted_iota(jnp.int32, full.shape, 0) == lax.broadcasted_iota(jnp.int32, full.shape, 1)
    picked = jnp.where(same, full, 0.0)
    down = jnp.sum(picked, axis=1, keepdims=True)
    across = jnp.sum(picked, axis=0, keepdims=True)
    denominators[0] = jnp.maximum(down + across - shift[p], denominator_floor)


def virtual_of(basis, energy, live, shift):
    pairs, projected, width = basis.shape
    return pl.pallas_call(
        virtual_kernel,
        out_shape=(
            jax.ShapeDtypeStruct((pairs, width, width), jnp.bfloat16),
            jax.ShapeDtypeStruct((pairs, width, width), jnp.float32),
        ),
        grid_spec=pltpu.PrefetchScalarGridSpec(
            num_scalar_prefetch=2,
            grid=(pairs,),
            in_specs=[
                pl.BlockSpec((1, projected, width), lambda p, *_: (p, 0, 0)),
                pl.BlockSpec((projected, 1), lambda p, *_: (0, 0)),
            ],
            out_specs=[pl.BlockSpec((1, width, width), lambda p, *_: (p, 0, 0))] * 2,
        ),
        cost_estimate=pl.CostEstimate(flops=2 * pairs * projected * width * width, bytes_accessed=4 * pairs * projected * width, transcendentals=0),
    )(live, shift, basis, energy)


def overlap_kernel(base, half, valid, pair, index, live, live_partner, own, twin, partner, *rest):
    n = pl.program_id(0)
    out = rest[-1]
    entry = base + n

    def product(mine):
        full = lax.dot_general(mine[0], partner[0], (((0,), (0,)), ((), ())), preferred_element_type=jnp.float32)
        both = live_rows(full.shape, live[entry]) & live_columns(full.shape, live_partner[entry])
        out[0] = jnp.where(both, full, 0.0).astype(jnp.bfloat16)

    @pl.when((valid[entry] > 0) & (n < half))
    def _():
        product(own)

    @pl.when((valid[entry] > 0) & (n >= half))
    def _():
        product(twin)


def overlap_of(tables, place, count, total, offset, own, twin, partners, sofar):
    projected, width = partners.shape[1:]
    half = count // 2
    base = place * count
    in_specs = [
        pl.BlockSpec((1, projected, width), lambda n, v, p, *_: (p[base + jnp.minimum(n, half - 1)], 0, 0)),
        pl.BlockSpec((1, projected, width), lambda n, v, p, *_: (p[base + jnp.maximum(n, half)], 0, 0)),
        pl.BlockSpec((1, projected, width), lambda n, v, p, k, *_: (k[base + n], 0, 0)),
    ]
    operands = [*tables, own, twin, partners]
    aliases = {}
    if sofar is not None:
        in_specs.append(pl.BlockSpec(memory_space=pl.ANY))
        aliases = {len(operands): 0}
        operands.append(sofar)
    return pl.pallas_call(
        functools.partial(overlap_kernel, base, half),
        out_shape=jax.ShapeDtypeStruct((total, width, width), jnp.bfloat16),
        grid_spec=pltpu.PrefetchScalarGridSpec(
            num_scalar_prefetch=5,
            grid=(count,),
            in_specs=in_specs,
            out_specs=pl.BlockSpec((1, width, width), lambda n, *_: (offset + n, 0, 0)),
        ),
        input_output_aliases=aliases,
        cost_estimate=pl.CostEstimate(
            flops=2 * count * projected * width * width, bytes_accessed=4 * count * projected * width, transcendentals=0
        ),
        name="overlap" + str(place),
    )(*operands)


def coupled_kernel(places, slots, who, valid, pair, index, weights, overlap, far_before, far_after, *rest):
    rounded, out = rest[:places], rest[places]
    total = rest[places + 1] if len(rest) > places + 1 else out
    total[...] = jnp.zeros_like(total)
    for place in range(places):
        for slot in range(slots):
            within = who * slots + slot
            entry = place * 2 * slots + within

            @pl.when(valid[entry] > 0)
            def _(place=place, entry=entry, within=within):
                if place == places - 2:
                    left = far_before[within]
                elif place == places - 1:
                    left = far_after[within]
                else:
                    left = overlap[entry]
                first = jnp.dot(left, rounded[place][index[entry]], preferred_element_type=jnp.float32)
                second = lax.dot_general(
                    first.astype(jnp.bfloat16), left, (((1,), (1,)), ((), ())), preferred_element_type=jnp.float32
                )
                total[pair[entry]] += weights[entry] * second

    if total is not out:
        out[...] = total[...].astype(out.dtype)


def coupled_of(who, slots, valid, pair, index, weights, overlaps, rounded):
    places = len(rounded)
    shape = rounded[0].shape
    kind = jnp.float32 if who == 0 else jnp.bfloat16
    smem = pl.BlockSpec(memory_space=pltpu.SMEM)
    vmem = pl.BlockSpec(memory_space=pltpu.VMEM)
    return pl.pallas_call(
        functools.partial(coupled_kernel, places, slots, who),
        out_shape=jax.ShapeDtypeStruct(shape, kind),
        in_specs=[smem] * 4 + [vmem] * (3 + places),
        out_specs=vmem,
        scratch_shapes=[pltpu.VMEM(shape, jnp.float32)] if who else [],
        cost_estimate=pl.CostEstimate(
            flops=4 * places * slots * shape[1] ** 3, bytes_accessed=places * 1500000, transcendentals=0
        ),
        name="coupled" + str(who),
    )(valid, pair, index, weights, *overlaps, *rounded)


def update_kernel(live, shift, own, other, virtual, denominators, current, integrals, update, squares):
    p = pl.program_id(0)
    rounded = current[0].astype(jnp.bfloat16)
    residual = integrals[0] + jnp.dot(virtual[0], rounded, preferred_element_type=jnp.float32)
    residual = residual + jnp.dot(rounded, virtual[0], preferred_element_type=jnp.float32)
    residual = residual - shift[p] * current[0] - (own[0] + other[0].astype(jnp.float32))
    both = live_rows(residual.shape, live[p]) & live_columns(residual.shape, live[p])
    change = jnp.where(both, residual, 0.0) / denominators[0]
    update[0] = change
    squared = change * change
    height, width = squared.shape
    part = jnp.sum(squared.reshape(height // 8, 8, width), axis=0)
    folded = part[:, :128]
    for start in range(128, width, 128):
        folded = folded + part[:, start : start + 128]

    @pl.when(p == 0)
    def _():
        squares[...] = folded

    @pl.when(p > 0)
    def _():
        squares[...] += folded


def update_of(live, shift, own, other, virtual, denominators, current, integrals):
    pairs, width, _ = current.shape
    wide = pl.BlockSpec((1, width, width), lambda p, *_: (p, 0, 0))
    return pl.pallas_call(
        update_kernel,
        out_shape=(
            jax.ShapeDtypeStruct((pairs, width, width), jnp.float32),
            jax.ShapeDtypeStruct((8, 128), jnp.float32),
        ),
        grid_spec=pltpu.PrefetchScalarGridSpec(
            num_scalar_prefetch=2,
            grid=(pairs,),
            in_specs=[wide] * 6,
            out_specs=[wide, pl.BlockSpec((8, 128), lambda p, *_: (0, 0))],
        ),
    )(live, shift, own, other, virtual, denominators, current, integrals)


def onward(x, groups):
    return lax.ppermute(x, "ia", [(i, i + 2) for i in range(groups - 2)])


def backward(x, groups):
    return lax.ppermute(x, "ia", [(i + 2, i) for i in range(groups - 2)])


def along_line(x, groups):
    before, after, found = x, x, [x]
    for _ in range(1, groups // 2):
        before, after = onward(before, groups), backward(after, groups)
        found += [before, after]
    return found


def shards(basis, amplitudes, integrals, virt_energy, fock, occ_energy, blocks, couplings):
    rows_here, columns_here, projected, pair_width = basis.shape
    pairs_here = rows_here * columns_here
    requests = NCOUPLE * pairs_here
    row_groups = lax.axis_size("ia")
    column_groups = lax.axis_size("ja")
    slot_count = requests // row_groups
    group_index = lax.axis_index("ia")
    first_row = group_index * rows_here
    total_pairs = rows_here * row_groups * columns_here * column_groups
    live = lax.dynamic_slice_in_dim(blocks, first_row, rows_here, 0).reshape(pairs_here) * BLOCK
    orbital_index = jnp.arange(pair_width, dtype=jnp.int32)
    column_mask = orbital_index[None, :] < live[:, None]
    pair_mask = column_mask[:, :, None] & column_mask[:, None, :]
    twins = [(i, i ^ 1) for i in range(row_groups)]
    last = row_groups // 2 - 1
    seen = [(group_index, group_index)] + [
        (group_index, group_index + sign * 2 * step) for step in range(1, last + 1) for sign in (-1, 1)
    ]
    places = len(seen)
    seen.append((group_index + 2, group_index - 2 * (last - 1)))
    seen.append((group_index - 2, group_index + 2 * (last - 1)))
    groups = jnp.stack([group for _, group in seen])
    requesters = jnp.stack([asking for asking, _ in seen])
    exists = (requesters >= 0) & (requesters < row_groups)
    requesters = jnp.clip(requesters, 0, row_groups - 1)
    requesters = jnp.stack([requesters, requesters ^ 1], axis=1)
    asked = couplings.reshape(row_groups, requests)[requesters]
    targets = asked // rows_here
    ranks = rank_within(targets)
    entry = jnp.arange(requests, dtype=jnp.int32)
    entry_pair = jnp.broadcast_to(entry // NCOUPLE, asked.shape)
    entry_column = entry_pair % columns_here
    entry_row = requesters[:, :, None] * rows_here + entry_pair // columns_here
    chosen = (
        (targets[:, :, None, :] == groups[:, None, None, None])
        & (ranks[:, :, None, :] == jnp.arange(slot_count, dtype=jnp.int32)[None, None, :, None])
        & exists[:, None, None, None]
    )

    def listed(values):
        return jnp.sum(jnp.where(chosen, values[:, :, None, :], 0), axis=-1).reshape(-1)

    rows_all = jnp.arange(fock.shape[0], dtype=jnp.int32)
    columns_all = jnp.arange(columns_here, dtype=jnp.int32)
    is_row = entry_row[..., None] == rows_all
    is_partner = asked[..., None] == rows_all
    is_column = entry_column[..., None] == columns_all
    fock_entry = jnp.sum(
        jnp.where(is_row[..., :, None] & is_partner[..., None, :], fock, 0.0), axis=(-2, -1)
    )
    live_entry = BLOCK * jnp.sum(
        jnp.where(is_row[..., :, None] & is_column[..., None, :], blocks, 0), axis=(-2, -1)
    )
    live_other = BLOCK * jnp.sum(
        jnp.where(is_partner[..., :, None] & is_column[..., None, :], blocks, 0), axis=(-2, -1)
    )
    valid = listed(jnp.ones_like(asked))
    pair = listed(entry_pair)
    index = listed((asked % rows_here) * columns_here + entry_column)
    weights = listed(fock_entry)
    live_rows_of = listed(live_entry)
    live_columns_of = listed(live_other)
    occupied_diag = lax.dynamic_slice_in_dim(jnp.diagonal(fock), first_row, rows_here, 0)
    shift = (occupied_diag[:, None] + occ_energy[None, :]).reshape(pairs_here)
    bases = basis.reshape(pairs_here, projected, pair_width)
    current = jnp.where(pair_mask, amplitudes.reshape(pairs_here, pair_width, pair_width), 0.0)
    pair_integrals = integrals.reshape(pairs_here, pair_width, pair_width)
    each = 2 * slot_count
    direct = places - 2
    tables = (valid, pair, index, live_rows_of, live_columns_of)
    twin = lax.ppermute(bases, "ia", twins)
    line_bases, before, after = [bases], bases, bases
    rounded = [current.astype(jnp.bfloat16)]
    earlier, later = onward(rounded[0], row_groups), backward(rounded[0], row_groups)
    rounded += [earlier, later]
    overlap, twin_before, twin_after, done = None, None, None, 0
    virtual, denominators = virtual_of(bases, virt_energy[:, None], live, shift)
    for step in range(1, last):
        before, after = onward(before, row_groups), backward(after, row_groups)
        if step > 1:
            while done < 2 * step - 1:
                overlap = overlap_of(
                    tables, done, each, direct * each, done * each, bases, twin, line_bases[done], overlap
                )
                done += 1
            earlier, later, overlap = lax.optimization_barrier((earlier, later, overlap))
            earlier, later = onward(earlier, row_groups), backward(later, row_groups)
            rounded += [earlier, later]
            before, after, overlap = lax.optimization_barrier((before, after, overlap))
        if step == 1:
            low, high = 2, row_groups - 4
            twin_before = lax.ppermute(before, "ia", [(low, low + 1), (low + 1, low)])
            twin_after = lax.ppermute(after, "ia", [(high, high + 1), (high + 1, high)])
        line_bases += [before, after]
    far_before = overlap_of(tables, places, each, each, 0, line_bases[2], twin_after, before, None)
    far_after = overlap_of(tables, places + 1, each, each, 0, line_bases[1], twin_before, after, None)
    far_before, far_after, overlap = lax.optimization_barrier((far_before, far_after, overlap))
    far_before, far_after = onward(far_before, row_groups), backward(far_after, row_groups)
    rounded += [onward(earlier, row_groups), backward(later, row_groups)]
    while done < direct:
        overlap = overlap_of(tables, done, each, direct * each, done * each, bases, twin, line_bases[done], overlap)
        done += 1
    overlaps = (overlap, far_before, far_after)
    for sweep_index in range(SWEEPS):
        if sweep_index:
            rounded = along_line(current.astype(jnp.bfloat16), row_groups)
        lists = (valid, pair, index, weights, overlaps, rounded)
        other = lax.ppermute(coupled_of(1, slot_count, *lists), "ia", twins)
        own = coupled_of(0, slot_count, *lists)
        update, squares = update_of(live, shift, own, other, virtual, denominators, current, pair_integrals)
        squares = jnp.sum(total_of(squares, row_groups, column_groups, sweep_index))
        factor = jnp.minimum(1.0, clip_share * pair_width / jnp.sqrt(squares / total_pairs + 1e-06))
        current = current - factor * update
    return current.reshape(rows_here, columns_here, pair_width, pair_width)


def solution(mesh):
    return jax.shard_map(
        shards,
        mesh=mesh,
        in_specs=(
            P("ia", "ja", None, None),
            P("ia", "ja", None, None),
            P("ia", "ja", None, None),
            P(),
            P(),
            P("ja"),
            P(None, "ja"),
            P(None, "ja", None),
        ),
        out_specs=P("ia", "ja", None, None),
        check_vma=False,
    )
```
